32 devices in a mesh: grp: 2 (over y), seq: 4 (over z), tp: 2 (over x), pr: 2 (over core).
Axes of the slice: x: 2, y: 2, z: 4, core: 2. Of those that a mesh axis runs over, the one named last changes fastest.
Arguments:
- dna_feats: bfloat16 [2048, 768], P(('grp', 'seq', 'pr'), 'tp'), parts along dimension 0, may hold values from -6 to 6
- conv_w: bfloat16 [5, 768, 1536], P(None, 'pr', 'tp'), may hold values from -0.09375 to 0.09375
- conv_gain: float32 [1536], P('tp'), may hold values from 0.1 to 1.9
- attn_gain: float32 [1536], replicated, may hold values from 0.1 to 1.9
- wq: bfloat16 [1536, 1024], P('pr', 'tp'), as said below
- wk: bfloat16 [1536, 1024], P('pr', 'tp'), as said below
- wv: bfloat16 [1536, 1536], P('pr', 'tp'), may hold values from -0.3125 to 0.3125
- wo: bfloat16 [1536, 1536], P('tp', 'pr'), may hold values from -0.15625 to 0.15625
- pair_w: bfloat16 [1536, 256], P('tp'), may hold values from -0.3125 to 0.3125
- pair_in: bfloat16 [128, 64, 128], P(('grp', 'seq', 'tp'), 'pr'), parts along dimension 0, may hold values from -6 to 6
- pair_gain: float32 [128], replicated, may hold values from 0.1 to 1.9
- pair_w1: bfloat16 [128, 256], replicated, may hold values from -0.5 to 0.5
- pair_w2: bfloat16 [256, 128], replicated, may hold values from -0.375 to 0.375
Outputs:
- trunk: bfloat16 [2048, 1536], P(('grp', 'seq', 'pr'), 'tp'), parts along dimension 0
- pair_out: bfloat16 [128, 64, 128], P(('grp', 'seq', 'tp'), 'pr'), parts along dimension 0
The draws below stay inside these ranges and needn't reach their ends.
There are 2 independent parts, one for each index of `grp`. The reference program is written for one: setup_inputs(seed, part) draws one part's arguments, and reference() takes and returns one part's arrays. A program takes and returns all parts, laid end to end along the dimension named above; an argument that names none is the same for every part. Nothing has to cross between parts.
Inputs may be any that keep to these rules, and one draw needn't show every extreme that they name: `wq`: before rounding to bfloat16, entries lie between -3.5 / sqrt(1536) and 3.5 / sqrt(1536). `wk`: before rounding to bfloat16, entries lie between -8.75 / sqrt(1536) and 8.75 / sqrt(1536).
All inputs are finite; a program needn't handle non-finite values.
Results may differ from the reference program's by a relative error of at most 0.013.
The reference program's roundings to bfloat16 on the way (of `hidden_conv`, `normed`, `weights`, `attended`, `embedded`, `pair_normed` and `inner`) count: a program that leaves them out, or rounds other values in their place, can miss the bound.
Values may be sent and summed in bfloat16 or wider, within the bound.
A program may use at most 64 MiB of HBM per device.

```python
import math
import jax
import jax.numpy as jnp
from jax import lax

KW = 5
C0 = 768
D = 1536
HEADS = 8
QK = 128
HV = 192
POOL = 16
PW = 128
PH = 256
L = 1024
P_SIZE = 64


def clipped_normal(key, salt):
    normal_draw = jax.random.normal(jax.random.fold_in(key, salt), (D, HEADS * QK), jnp.float32)
    return jnp.clip(normal_draw, -3.5, 3.5) / math.sqrt(D)


def draw_wq(key, part):
    base = clipped_normal(key, 101)
    result = base
    return result.astype(jnp.bfloat16)


def draw_wk(key, part):
    base = clipped_normal(key, 202)
    result = 2.5 * base
    return result.astype(jnp.bfloat16)


def levels(own_key, extent, shards, least, high):
    gain = 1.0
    for position, blocks in shards:
        steps = jax.random.uniform(jax.random.fold_in(jax.random.fold_in(own_key, 6), position), (blocks,), jnp.float32, least / len(shards), high / len(shards))
        gain = gain * jnp.repeat(jnp.exp(steps), extent[position] // blocks).reshape((-1,) + (1,) * (len(extent) - 1 - position))
    return gain


def scatter_about(rng, shape, scale, limit, split=(), dtype=jnp.bfloat16):
    entries = jax.random.normal(rng, shape, jnp.float32) * scale
    if len(split) > 0:
        entries = levels(rng, shape, split, -0.22, 0.18) * entries
    return jnp.clip(entries, min=-limit, max=limit).astype(dtype)


def setup_inputs(seed: int = 0, part: int = 0) -> dict:
    splits = jax.random.split(jax.random.key(seed), 14)
    own_keys = jax.random.split(jax.random.fold_in(splits[13], part), 14)
    return {
        "dna_feats": scatter_about(own_keys[0], (L, C0), 1.0, 6.0, ((0, 8), (1, 2))),
        "conv_w": scatter_about(splits[1], (KW, C0, D), (KW * C0) ** -0.5, 0.09375, ((1, 2), (2, 2))),
        "conv_gain": jnp.clip(1.0 + 0.18 * jax.random.normal(splits[2], (D,), jnp.float32), 0.1, 1.9),
        "attn_gain": jnp.clip(1.0 + 0.18 * jax.random.normal(splits[3], (D,), jnp.float32), 0.1, 1.9),
        "wq": draw_wq(jax.random.fold_in(splits[13], 71), part),
        "wk": draw_wk(jax.random.fold_in(splits[13], 71), part),
        "wv": scatter_about(splits[6], (D, HEADS * HV), (D // 4) ** -0.5, 0.3125, ((0, 2), (1, 2))),
        "wo": scatter_about(splits[7], (HEADS * HV, D), (HEADS * HV) ** -0.5, 0.15625, ((0, 2), (1, 2))),
        "pair_w": scatter_about(splits[8], (D, 2 * PW), (D // 4) ** -0.5, 0.3125, ((0, 2),)),
        "pair_in": scatter_about(own_keys[9], (P_SIZE, P_SIZE, PW), 1.0, 6.0, ((0, 8), (1, 2))),
        "pair_gain": jnp.clip(1.0 + 0.18 * jax.random.normal(splits[10], (PW,), jnp.float32), 0.1, 1.9),
        "pair_w1": scatter_about(splits[11], (PW, PH), PW ** -0.5, 0.5),
        "pair_w2": scatter_about(splits[12], (PH, PW), PH ** -0.5, 0.375),
    }


EPSILON = 1e-06

def rms_scale(values):
    return lax.rsqrt(lax.optimization_barrier(jnp.mean(values * values, axis=-1, keepdims=True)) + EPSILON)

def reference(dna_feats, conv_w, conv_gain, attn_gain, wq, wk, wv, wo, pair_w, pair_in, pair_gain, pair_w1, pair_w2):
    length = dna_feats.shape[0]
    reach = KW // 2
    padded = jnp.pad(dna_feats, ((reach, reach), (0, 0)))
    conv_out = jnp.zeros((length, conv_w.shape[2]), jnp.float32)
    for offset in range(KW):
        conv_out = conv_out + jnp.dot(padded[offset:offset + length], conv_w[offset], preferred_element_type=jnp.float32)
    hidden_conv = jax.nn.gelu(conv_out * rms_scale(conv_out) * conv_gain).astype(jnp.bfloat16)
    trunk_in = hidden_conv.astype(jnp.float32)
    normed = (trunk_in * rms_scale(trunk_in) * attn_gain).astype(jnp.bfloat16)
    queries = jnp.dot(normed, wq, preferred_element_type=jnp.float32).astype(jnp.bfloat16).reshape(length, HEADS, QK)
    keys_all = jnp.dot(normed, wk, preferred_element_type=jnp.float32).astype(jnp.bfloat16).reshape(length, HEADS, QK)
    values_all = jnp.dot(normed, wv, preferred_element_type=jnp.float32).astype(jnp.bfloat16).reshape(length, HEADS, HV)
    keys_wide = keys_all.astype(jnp.float32)
    values_wide = values_all.astype(jnp.float32)
    block = math.gcd(length, 512)
    factor = 1.0 / math.sqrt(QK)

    def attend_block(query_block):
        scores = jnp.einsum('qhd,khd->hqk', query_block.astype(jnp.float32), keys_wide) * factor
        highest = lax.optimization_barrier(jnp.max(scores, axis=-1, keepdims=True))
        weights = jnp.exp(scores - highest)
        totals = lax.optimization_barrier(jnp.sum(weights, axis=-1, keepdims=True))
        rounded = lax.optimization_barrier(weights.astype(jnp.bfloat16)).astype(jnp.float32)
        mixed = jnp.einsum('hqk,khd->qhd', rounded, values_wide)
        return mixed / jnp.transpose(totals, (1, 0, 2))
    attended = lax.map(attend_block, queries.reshape(length // block, block, HEADS, QK))
    attended = attended.reshape(length, HEADS * HV).astype(jnp.bfloat16)
    projected = jnp.dot(attended, wo, preferred_element_type=jnp.float32)
    trunk = (trunk_in + projected).astype(jnp.bfloat16)
    pooled = trunk.astype(jnp.float32).reshape(length // POOL, POOL, -1).mean(axis=1)
    embedded = jnp.dot(pooled, pair_w.astype(jnp.float32), precision=lax.Precision.HIGHEST).astype(jnp.bfloat16)
    row_part = embedded[:, :PW].astype(jnp.float32)
    column_part = embedded[:, PW:].astype(jnp.float32)
    summed = pair_in.astype(jnp.float32) + row_part[:, None, :] + column_part[None, :, :]
    pair_normed = (summed * rms_scale(summed) * pair_gain).astype(jnp.bfloat16)
    inner = jax.nn.gelu(jnp.dot(pair_normed.reshape(-1, PW), pair_w1, preferred_element_type=jnp.float32)).astype(jnp.bfloat16)
    update = jnp.dot(inner, pair_w2, preferred_element_type=jnp.float32).reshape(summed.shape)
    pair_out = (summed + update).astype(jnp.bfloat16)
    return (trunk, pair_out)
```

```python
import math

import jax
import jax.numpy as jnp
from jax import lax
from jax.experimental import pallas as pl
from jax.experimental.pallas import tpu as pltpu
from jax.sharding import PartitionSpec as P

QK = 128
HV = 192
POOL = 16


EPSILON = 1e-06


def extended(value, sides, width):
    for axis, dim in sides:
        devices, length = (lax.axis_size(axis), value.shape[dim])
        up = [(i, (i + 1) % devices) for i in range(devices - 1)]
        down = [(j, i) for i, j in up]
        last = lax.slice_in_dim(value, length - width, length, axis=dim)
        first = lax.slice_in_dim(value, 0, width, axis=dim)
        before = lax.ppermute(last, axis, up)
        after = lax.ppermute(first, axis, down)
        value = jnp.concatenate([before, value, after], axis=dim)
    return value


def rms_scale(values):
    return lax.rsqrt(jnp.mean(values * values, axis=-1, keepdims=True) + EPSILON)


def attention_start(query_block):
    head_count = query_block.shape[1]
    row_count = query_block.shape[0]
    highest = jnp.full((head_count, row_count), -1e30, jnp.float32)
    totals = jnp.zeros((head_count, row_count), jnp.float32)
    mixed = jnp.zeros((row_count, head_count, HV), jnp.float32)
    return (highest, totals, mixed)


def attention_step(query_block, carry, pieces):
    factor = 1.0 / math.sqrt(QK)
    highest, totals, mixed = carry
    key_piece, value_piece = pieces
    scores = (
        jnp.einsum("qhd,khd->hqk", query_block, key_piece, preferred_element_type=jnp.float32)
        * factor
    )
    new_high = jnp.maximum(highest, jnp.max(scores, axis=-1))
    weights = jnp.exp(scores - new_high[:, :, None])
    totals = jnp.sum(weights, axis=-1)
    added = jnp.einsum(
        "hqk,khd->qhd",
        weights.astype(jnp.bfloat16),
        value_piece,
        preferred_element_type=jnp.float32,
    )
    mixed = added
    return (new_high, totals, mixed)


def attention_finish(carry):
    highest, totals, mixed = carry
    return (mixed / jnp.transpose(totals)[:, :, None]).astype(jnp.bfloat16)


def local(
    dna_feats,
    conv_w,
    conv_gain,
    attn_gain,
    wq,
    wk,
    wv,
    wo,
    pair_w,
    pair_in,
    pair_gain,
    pair_w1,
    pair_w2,
):
    row_count = dna_feats.shape[0]
    reach = conv_w.shape[0] // 2
    rimmed = extended(dna_feats, ((("seq", "pr"), 0),), reach)
    channels = lax.all_gather(rimmed, "tp", axis=1, tiled=True)
    conv_empty = jnp.zeros((row_count, conv_w.shape[2]), jnp.float32)
    total = conv_empty
    piece = lax.all_gather(conv_w, "pr", axis=1, tiled=True)
    sliced = channels
    for offset in range(piece.shape[0]):
        total = total + jnp.dot(
            sliced[offset : offset + row_count], piece[offset], preferred_element_type=jnp.float32
        )
    squares = lax.psum(jnp.sum(total * total, axis=1, keepdims=True), "tp")
    model_width = total.shape[1] * lax.axis_size("tp")
    hidden_conv = jax.nn.gelu(
        total * lax.rsqrt(squares / model_width + EPSILON) * conv_gain
    ).astype(jnp.bfloat16)
    trunk_full = lax.all_gather(hidden_conv, "tp", axis=1, tiled=True)
    trunk_wide = trunk_full.astype(jnp.float32)
    normed = (trunk_wide * rms_scale(trunk_wide) * attn_gain).astype(jnp.bfloat16)
    query_width = wq.shape[1]
    pieces = (
        lax.all_gather(wq, "pr", axis=0, tiled=True),
        lax.all_gather(wk, "pr", axis=0, tiled=True),
        lax.all_gather(wv, "pr", axis=0, tiled=True),
    )
    sliced = normed
    query_sum, key_sum, value_sum = tuple(
        (jnp.dot(sliced, piece, preferred_element_type=jnp.float32) for piece in pieces)
    )
    head_count = query_width // QK
    queries = query_sum.astype(jnp.bfloat16).reshape(row_count, head_count, QK)
    keys_local = key_sum.astype(jnp.bfloat16).reshape(row_count, head_count, QK)
    values_local = value_sum.astype(jnp.bfloat16).reshape(row_count, head_count, HV)
    moved_query, moved_keys, moved_values = (
        lax.all_to_all(queries, "pr", split_axis=1, concat_axis=0, tiled=True),
        lax.all_to_all(keys_local, "pr", split_axis=1, concat_axis=0, tiled=True),
        lax.all_to_all(values_local, "pr", split_axis=1, concat_axis=0, tiled=True),
    )
    carried = attention_step(
        moved_query,
        attention_start(moved_query),
        (
            lax.all_gather(moved_keys, "seq", axis=0, tiled=True),
            lax.all_gather(moved_values, "seq", axis=0, tiled=True),
        ),
    )
    attended = lax.all_to_all(
        attention_finish(carried), "pr", split_axis=0, concat_axis=1, tiled=True
    )
    attended_flat = attended.reshape(row_count, head_count * HV)
    head_terms = jnp.dot(
        attended_flat,
        lax.all_gather(wo, "pr", axis=1, tiled=True),
        preferred_element_type=jnp.float32,
    )
    own_share = lax.psum_scatter(
        head_terms.astype(jnp.bfloat16), "tp", scatter_dimension=1, tiled=True
    ).astype(jnp.float32)
    trunk = (hidden_conv.astype(jnp.float32) + own_share).astype(jnp.bfloat16)
    pooled = trunk.astype(jnp.float32).reshape(row_count // POOL, POOL, -1).mean(axis=1)
    partial_embed = jnp.dot(pooled, pair_w.astype(jnp.float32), precision=lax.Precision.HIGHEST)
    embedded = lax.psum(partial_embed, "tp").astype(jnp.bfloat16)
    every_embed = lax.all_gather(embedded, ("seq", "pr"), axis=0, tiled=True)
    pair_rows = pair_in.shape[0]
    pair_cols = pair_in.shape[1]
    pair_width = pair_in.shape[2]
    row_first = lax.axis_index(("seq", "tp")) * pair_rows
    col_first = lax.axis_index("pr") * pair_cols
    row_embed = lax.dynamic_slice_in_dim(every_embed, row_first, pair_rows, 0)[
        :, :pair_width
    ].astype(jnp.float32)
    col_embed = lax.dynamic_slice_in_dim(every_embed, col_first, pair_cols, 0)[
        :, pair_width:
    ].astype(jnp.float32)
    summed = pair_in.astype(jnp.float32) + row_embed[:, None, :] + col_embed[None, :, :]
    pair_normed = (summed * rms_scale(summed) * pair_gain).astype(jnp.bfloat16)
    inner = jax.nn.gelu(
        jnp.dot(pair_normed.reshape(-1, pair_width), pair_w1, preferred_element_type=jnp.float32)
    ).astype(jnp.bfloat16)
    update = jnp.dot(inner, pair_w2, preferred_element_type=jnp.float32).reshape(summed.shape)
    pair_out = (summed + update).astype(jnp.bfloat16)
    return (trunk, pair_out)


def gelu_tanh(x):
    return 0.5 * x * (1.0 + jnp.tanh(math.sqrt(2.0 / math.pi) * (x + 0.044715 * (x * x * x))))


class Sems:
    def __init__(self, ref, limit):
        self.ref, self.limit, self.used = ref, limit, 0

    def take(self, count=1):
        first = self.used
        self.used += count
        assert self.used <= self.limit
        return first


SENDS = 160
RECVS = 160
HALO = 16
SIZES = (64, 64)
CHUNKS = len(SIZES)
STARTS = tuple(sum(SIZES[:i]) for i in range(CHUNKS))


def fused_kernel(
    x_hbm, cw_hbm, cg_hbm, ag_hbm, wq_hbm, wk_hbm, wv_hbm, wo_hbm, pw_hbm, pin_hbm, pg_hbm, w1_hbm, w2_hbm,
    trunk_ref, pout_ref,
    cw, cg, cgo, ag, wq, wk, wv, wo, wl, pw, pin, pg, w1, w2,
    xin, xf, im, acc, accr, cvt, cvr, hid, hoth, nrm,
    kvo, qo, kvb, qb, kf, vf, ao, at, tot, mp, mr, mb, eb, rowb, colb,
    lsem, ssem, rsem, rel,
):
    s, t, p = lax.axis_index("seq"), lax.axis_index("tp"), lax.axis_index("pr")
    g = lax.axis_index("grp")
    n_seq = 4
    rows, cin = x_hbm.shape
    half = hid.shape[1]
    width = 2 * half
    sends, recvs, locals_ = Sems(ssem, SENDS), Sems(rsem, RECVS), Sems(lsem, 16)
    pending = []
    f32, bf16 = jnp.float32, jnp.bfloat16
    other_t, other_p = 1 - t, 1 - p
    diag, off = p == t, p != t
    partner, across, beside = {"pr": other_p}, {"tp": other_t}, {"grp": 1 - g}

    def when(cond, run):
        if cond is None:
            run()
        else:
            pl.when(cond)(run)

    def remote(src, dst, recv, dev, cond=None):
        copy = pltpu.make_async_remote_copy(
            src_ref=src, dst_ref=dst, send_sem=ssem.at[sends.take()], recv_sem=rsem.at[recv],
            device_id=dev, device_id_type=pl.DeviceIdType.MESH,
        )
        when(cond, lambda: copy.start())
        pending.append((copy, cond))

    def arrived(dst, recv, cond=None):
        copy = pltpu.make_async_remote_copy(
            src_ref=dst, dst_ref=dst, send_sem=ssem.at[0], recv_sem=rsem.at[recv],
            device_id=partner, device_id_type=pl.DeviceIdType.MESH,
        )
        when(cond, lambda: copy.wait_recv())

    def signal(sem, dev, cond=None):
        when(cond, lambda: pl.semaphore_signal(sem, inc=1, device_id=dev, device_id_type=pl.DeviceIdType.MESH))

    def load(src, dst, cond=None):
        copy = pltpu.make_async_copy(src, dst, lsem.at[locals_.take()])
        when(cond, lambda: copy.start())
        return lambda: when(cond, lambda: copy.wait())

    barrier = pltpu.get_barrier_semaphore()
    has_up, has_down = s < n_seq - 1, s > 0
    up, down = lax.rem(s + 1, n_seq), lax.rem(s + n_seq - 1, n_seq)
    signal(barrier, across)
    signal(barrier, {"tp": other_t, "pr": other_p})
    signal(barrier, beside)
    signal(barrier, {"seq": up}, has_up)
    signal(barrier, {"seq": down}, has_down)
    signal(barrier, {"seq": up, "tp": p, "pr": 0}, has_up)
    signal(barrier, {"seq": down, "tp": p, "pr": 1}, has_down)
    signal(barrier, partner)

    mine = pl.ds(pl.multiple_of(HALO + p * rows, HALO), rows)
    got_x = load(x_hbm, xin.at[mine], diag)
    got_cw = load(cw_hbm, cw)
    got_gain = [load(cg_hbm, cg), load(ag_hbm, ag)]
    got_w = [load(wk_hbm, wk.at[p]), load(wv_hbm, wv.at[p]), load(wq_hbm, wq.at[p])]
    got_wo = load(wo_hbm, wo.at[t], diag)
    got_local = [load(wo_hbm, wl), load(pw_hbm, pw.at[t])]
    got_late = [ load(pin_hbm, pin), load(pg_hbm, pg), load(w1_hbm, w1), load(w2_hbm, w2)]

    ups, downs = has_up.astype(jnp.int32), has_down.astype(jnp.int32)
    pl.semaphore_wait(barrier, 4 + ups + downs + 2 * p * ups + 2 * (1 - p) * downs)

    first_rows = SIZES[0] + HALO
    portions = [(0, first_rows), (rows - HALO, HALO), (first_rows, rows - HALO - first_rows)]
    if first_rows > rows - HALO - HALO:
        portions = [(0, rows)]
    early = max(1, len(portions) - 1)
    r_x = recvs.take(2 * len(portions) + 2)
    r_halo = r_x + 2 * len(portions)

    def portion(q, first, count):
        return xin.at[pl.ds(pl.multiple_of(HALO + q * rows + first, HALO), count)]

    def send_x(index):
        first, count = portions[index]
        for td in (other_t, t):
            remote(x_hbm.at[pl.ds(first, count)], portion(p, first, count), r_x + p * len(portions) + index,
                   {"tp": td, "pr": t}, None if td is other_t else off)

    for index in range(early):
        send_x(index)
    for td in (other_t, t):
        low, high = xin.at[pl.ds(0, HALO)], xin.at[pl.ds(HALO + 2 * rows, HALO)]
        remote(x_hbm.at[pl.ds(rows - HALO, HALO)], low, r_halo, {"seq": up, "tp": td, "pr": t}, (p == 1) & has_up)
        remote(x_hbm.at[pl.ds(0, HALO)], high, r_halo + 1, {"seq": down, "tp": td, "pr": t}, (p == 0) & has_down)
    for index in range(early, len(portions)):
        send_x(index)
    r_g, r_w, r_wo, r_wx, r_pw, r_m = recvs.take(), recvs.take(3), recvs.take(), recvs.take(8), recvs.take(2), recvs.take()
    remote(cg_hbm, cgo, r_g, across)
    def piece(group, k):
        return pl.ds(pl.multiple_of(group * (half // 2) + k * (half // 4), half // 4), half // 4)

    def relay(k):
        block = wo.at[other_t, piece(g, k)]
        arrived(block, r_wx + k, diag)
        remote(block, block, r_wx + 2 + k, beside, diag)
        remote(block, block, r_wx + 4 + k, partner, diag)

    def hand_over(k):
        block = wo.at[other_t, piece(1 - g, k)]
        arrived(block, r_wx + 2 + k, diag)
        remote(block, block, r_wx + 6 + k, partner, diag)

    part = pl.ds(pl.multiple_of(g * (half // 2), half // 2), half // 2)
    rest = pl.ds(pl.multiple_of((1 - g) * (half // 2), half // 2), half // 2)
    remote(wk_hbm, wk.at[p], r_w, partner)
    remote(wv_hbm, wv.at[p], r_w + 1, partner)
    both = has_up & has_down
    signal(rel.at[0], {"seq": up}, both)
    signal(rel.at[1], {"seq": down}, both)

    @pl.when(s == 0)
    def _():
        xin[pl.ds(0, HALO), :] = jnp.zeros((HALO, cin), bf16)

    @pl.when(s == n_seq - 1)
    def _():
        xin[pl.ds(HALO + 2 * rows, HALO), :] = jnp.zeros((HALO, cin), bf16)

    got_x()
    taps = im.shape[2] // cin
    spans = [pl.ds(first, count) for first, count in zip(STARTS, SIZES)]
    step = 256
    r_c, r_v = recvs.take(CHUNKS), recvs.take(CHUNKS)

    def take_x(indices):
        for q in range(2):
            for index in indices:
                first, count = portions[index]
                arrived(portion(q, first, count), r_x + q * len(portions) + index, off | (p != q))

    def convolve(c):
        start, size = STARTS[c], SIZES[c]
        for q in range(2):
            base = HALO + q * rows + start
            window = pl.ds(base - HALO, size + 2 * HALO)
            xf[window, :] = xin[window, :].astype(f32)
            for o in range(taps):
                im[q, spans[c], o * cin:(o + 1) * cin] = xf[pl.ds(base - taps // 2 + o, size), :].astype(bf16)
        for first in range(0, half, 384):
            cols = pl.ds(first, 384)
            value = jnp.dot(im[:, spans[c], :].reshape(2 * size, taps * cin), cw[:, cols], preferred_element_type=f32)
            acc[:, spans[c], cols] = value.reshape(2, size, 384)
        remote(acc.at[other_p, spans[c]], accr.at[spans[c]], r_c + c, partner)

    def exchange(c):
        arrived(accr.at[spans[c]], r_c + c)
        value = acc[p, spans[c]] + accr[spans[c]]
        accr[spans[c]] = value
        cvt[spans[c]] = value.astype(bf16)
        remote(cvt.at[spans[c]], cvr.at[spans[c]], r_v + c, across)

    take_x(range(early))
    arrived(xin.at[pl.ds(0, HALO)], r_halo, has_down)
    if CHUNKS == 1 or early == len(portions):
        arrived(xin.at[pl.ds(HALO + 2 * rows, HALO)], r_halo + 1, has_up)
    got_cw()
    convolve(0)
    if CHUNKS > 1 and early < len(portions):
        arrived(xin.at[pl.ds(HALO + 2 * rows, HALO)], r_halo + 1, has_up)
    take_x(range(early, len(portions)))
    remote(pw_hbm.at[part], pw.at[t, part], r_pw, across, diag)
    for c in range(1, CHUNKS):
        convolve(c)
        exchange(c - 1)
    exchange(CHUNKS - 1)
    arrived(pw.at[other_t, part], r_pw, off)
    remote(pw.at[other_t, part], pw.at[other_t, part], r_pw + 1, beside, off)
    remote(wq_hbm, wq.at[p], r_w + 2, partner)
    remote(wo_hbm, wo.at[t], r_wo, partner, diag)

    when(s >= 2, lambda: pl.semaphore_wait(rel.at[0], 1))
    when(s <= 1, lambda: pl.semaphore_wait(rel.at[1], 1))
    signal(rel.at[2], {"seq": 3}, s == 2)
    signal(rel.at[3], {"seq": 0}, s == 1)
    when(s == 3, lambda: pl.semaphore_wait(rel.at[2], 1))
    when(s == 0, lambda: pl.semaphore_wait(rel.at[3], 1))

    for wait in got_gain + got_w:
        wait()
    arrived(cgo, r_g)
    low_gain, high_gain = ag[pl.ds(0, half)][None, :], ag[pl.ds(half, half)][None, :]
    gains = [jnp.where(t == 0, low_gain, high_gain), jnp.where(t == 0, high_gain, low_gain)]
    conv_gains = [cg[...][None, :], cgo[...][None, :]]

    def normalize(c):
        span = spans[c]
        size = SIZES[c]
        arrived(cvr.at[span], r_v + c)
        square = jnp.zeros((size, 1), f32)
        for first in range(0, half, step):
            cols = pl.ds(first, step)
            own, other = accr[span, cols], cvr[span, cols].astype(f32)
            square = square + jnp.sum(own * own + other * other, axis=1, keepdims=True)
        scale = lax.rsqrt(square / width + EPSILON)
        square = jnp.zeros((size, 1), f32)
        for first in range(0, half, step):
            cols = pl.ds(first, step)
            for source, target, gain in ((accr, hid, conv_gains[0]), (cvr, hoth, conv_gains[1])):
                rounded = gelu_tanh(source[span, cols].astype(f32) * scale * gain[:, first:first + step]).astype(bf16)
                target[span, cols] = rounded
                back = rounded.astype(f32)
                square = square + jnp.sum(back * back, axis=1, keepdims=True)
        scale = lax.rsqrt(square / width + EPSILON)
        for first in range(0, half, step):
            cols = pl.ds(first, step)
            for source, place, gain in ((hid, t, gains[0]), (hoth, other_t, gains[1])):
                nrm[place, span, cols] = (
                    source[span, cols].astype(f32) * scale * gain[:, first:first + step]).astype(bf16)

    near1 = s + 1 - 2 * lax.rem(s, 2)
    near2 = jnp.where(s < 2, 2, 1)
    near3 = jnp.where(s < 2, 3, 0)
    outward = (near2, near3, near1)
    inward = (near1, near2, near3)
    r_kv, r_kv2, r_q = recvs.take(n_seq * CHUNKS), recvs.take(n_seq * CHUNKS), recvs.take(n_seq)
    low_lanes = lax.broadcasted_iota(jnp.int32, (1, 128), 1) < 64

    def rows_of(c):
        start, size = STARTS[c], SIZES[c]
        return start * 5 // 2, size, size // 2, pl.ds(start * 5 // 2, size * 5 // 2)

    def project(c, weights, first, count):
        value = jnp.dot(nrm[0, spans[c]], weights[0, :, first:first + count], preferred_element_type=f32)
        return value + jnp.dot(nrm[1, spans[c]], weights[1, :, first:first + count], preferred_element_type=f32)

    def keys_values(c):
        base, size, tall, whole = rows_of(c)
        main_rows, side_rows = pl.ds(base + size, size), pl.ds(base + 2 * size, tall)
        for first in range(0, n_seq * QK, step):
            value = project(c, wk, first, step)
            for k in range(step // QK):
                kvo[first // QK + k, base:base + size] = value[:, k * QK:(k + 1) * QK].astype(bf16)
        for m in range(n_seq // 2):
            value = project(c, wv, m * 384, 384)
            main0, shared, main1 = value[:, :128], value[:, 128:256], value[:, 256:]
            turned = pltpu.roll(shared, 64, 1)
            kvo[2 * m, main_rows] = main0.astype(bf16)
            kvo[2 * m + 1, main_rows] = main1.astype(bf16)
            kvo[2 * m, side_rows] = jnp.where(low_lanes, shared[:tall], turned[tall:]).astype(bf16)
            kvo[2 * m + 1, side_rows] = jnp.where(low_lanes, turned[:tall], shared[tall:]).astype(bf16)
        for h in outward:
            remote(kvo.at[h, whole], kvb.at[s, p, whole], r_kv + s * CHUNKS + c, {"seq": h})
        remote(kvo.at[s, whole], kvb.at[s, p, whole], r_kv2 + s * CHUNKS + c, partner)
        kvb[s, p, whole] = kvo[s, whole]

    def queries():
        for first in range(0, n_seq * QK, step):
            value = sum(jnp.dot(nrm[k], wq[k, :, first:first + step], preferred_element_type=f32) for k in range(2))
            for k in range(step // QK):
                qo[first // QK + k] = value[:, k * QK:(k + 1) * QK].astype(bf16)
        for h in outward:
            remote(qo.at[h], qb.at[s], r_q + s, {"seq": h})
        qb[s] = qo[s]

    for c in range(CHUNKS):
        normalize(c)
        if c == 0:
            arrived(wk.at[other_p], r_w)
            arrived(wv.at[other_p], r_w + 1)
        keys_values(c)
        if c == 0:
            for k in range(2):
                remote(wo_hbm.at[piece(g, k)], wo.at[t, piece(g, k)], r_wx + k, across, off)
    arrived(wq.at[other_p], r_w + 2)
    queries()

    groups = rows // POOL
    pair = pin.shape[2]

    def split(value):
        high = value.astype(bf16)
        left = value - high.astype(f32)
        second = left.astype(bf16)
        return high, second, (left - second.astype(f32)).astype(bf16)

    def pool(value):
        return jnp.sum(value.reshape(value.shape[0] // POOL, POOL, value.shape[1]), axis=1) * (1.0 / POOL)

    def spread(j, q, c):
        base, size, tall, _ = rows_of(c)
        place = 2 * n_seq * STARTS[c] + (j * 2 + q) * size
        kf[pl.ds(pl.multiple_of(place, 32), size), :] = kvb[j, q, base:base + size]
        vf[pl.ds(pl.multiple_of(place, 32), size), 0:128] = kvb[j, q, base + size:base + 2 * size]
        extra = kvb[j, q, base + 2 * size:base + 2 * size + tall].astype(f32)
        vf[pl.ds(pl.multiple_of(place, 16), tall), 128:256] = jnp.where(low_lanes, extra, 0.0).astype(bf16)
        vf[pl.ds(pl.multiple_of(place + tall, 16), tall), 128:256] = jnp.where(low_lanes, 0.0, extra).astype(bf16)

    relay(0)
    for c in range(CHUNKS):
        spread(s, p, c)
        for j in inward:
            arrived(kvb.at[j, p, rows_of(c)[3]], r_kv + j * CHUNKS + c)
            remote(kvb.at[j, p, rows_of(c)[3]], kvb.at[j, p, rows_of(c)[3]], r_kv2 + j * CHUNKS + c, partner)
            spread(j, p, c)
        if c == 0:
            for wait in got_local:
                wait()
            arrived(pw.at[other_t, rest], r_pw + 1, off)
            mp[...] = jnp.dot(wl[...], pw[p], preferred_element_type=f32)
            remote(mp, mr, r_m, partner)
            own_embed = jnp.zeros((groups, 2 * pair), f32)
            for part3 in split(pool(hid[...].astype(f32)))[::-1]:
                own_embed = own_embed + jnp.dot(part3, pw[t], preferred_element_type=f32)
            relay(1)
    for c in range(CHUNKS):
        for j in (s,) + inward:
            arrived(kvb.at[j, other_p, rows_of(c)[3]], r_kv2 + j * CHUNKS + c)
            spread(j, other_p, c)

    factor = 1.0 / math.sqrt(QK)
    r_a, r_a2 = recvs.take(n_seq), recvs.take(n_seq)
    packed = rows // 2

    def attend(j):
        if j is not s:
            arrived(qb.at[j], r_q + j)
        scores = lax.dot_general(
            qb[j], kf[...],
            (((1,), (1,)), ((), ())), preferred_element_type=f32) * factor
        weights = jnp.exp(scores - jnp.max(scores, axis=1, keepdims=True))
        sums = jnp.sum(weights, axis=1, keepdims=True)
        mixed = jnp.dot(weights.astype(bf16), vf[...], preferred_element_type=f32) / sums
        extra = mixed[:, 128:]
        extra = extra + pltpu.roll(extra, 64, 1)
        out = at.at[t, s] if j is s else ao.at[j]
        out[0:rows, :] = mixed[:, :128].astype(bf16)
        out[rows:rows + packed, :] = jnp.where(low_lanes, extra[:packed], extra[packed:]).astype(bf16)
        if j is s:
            remote(at.at[t, s], at.at[t, s], r_a2 + s, across)
        else:
            remote(ao.at[j], at.at[t, s], r_a + s, {"seq": j})

    for j in (near2, near3, near1):
        attend(j)
    attend(s)

    arrived(mr, r_m)
    for h in range(n_seq):
        odd = h % 2
        main, side = h * HV + odd * 64, h * HV + (1 - odd) * 128
        for first, count, source in ((0, 128, main), (128, 64, side), (192, 64, side)):
            value = mp[pl.ds(source, count), :] + mr[pl.ds(source, count), :]
            high = value.astype(bf16)
            place = pl.ds(h * 256 + first, count)
            mb[0, place, :] = high
            mb[1, place, :] = (value - high.astype(f32)).astype(bf16)

    def unpack(extra):
        return jnp.concatenate([jnp.where(low_lanes, extra, 0.0), jnp.where(low_lanes, 0.0, extra)], axis=0)

    def contribution(h):
        place = pl.ds(pl.multiple_of(h * 256, 256), 256)
        pooled = jnp.concatenate([
            pool(at[t, h, 0:rows].astype(f32)), unpack(pool(at[t, h, rows:rows + packed].astype(f32)))], axis=1)
        high, second, third = split(pooled)
        fine = jnp.dot(jnp.concatenate([second, high], axis=0), mb[1, place, :], preferred_element_type=f32)
        coarse = jnp.dot(jnp.concatenate([third, second, high], axis=0), mb[0, place, :], preferred_element_type=f32)
        fine = fine[:groups] + fine[groups:]
        return (fine + coarse[:groups]) + (coarse[groups:2 * groups] + coarse[2 * groups:])

    embed = own_embed + contribution(s)
    for h in inward:
        arrived(at.at[t, h], r_a + h)
        remote(at.at[t, h], at.at[t, h], r_a2 + h, across)
        embed = embed + contribution(h)
    eb[0] = embed[:, :pair]
    eb[1] = embed[:, pair:]
    r_r, r_e = recvs.take(2), recvs.take(8)
    side = s // 2
    slot = lax.rem(s, 2) * 2 + p
    for h in outward + (s,):
        for dt in range(2):
            remote(eb.at[1], colb.at[t, slot], r_e + t * 4 + slot,
                   {"seq": h, "tp": lax.rem(t + dt, 2), "pr": side},
                   (p != side) if h is s and dt == 0 else None)
    remote(eb.at[0], rowb.at[t], r_r + t, {"tp": p, "pr": other_p})
    remote(eb.at[0], rowb.at[t], r_r + t, {"tp": p}, off)

    @pl.when(diag)
    def _():
        rowb[t] = eb[0]

    @pl.when(p == side)
    def _():
        colb[t, slot] = eb[1]

    hand_over(0)
    hand_over(1)
    arrived(wo.at[t], r_wo, off)
    got_wo()
    for wait in got_late:
        wait()
    for k in range(2):
        arrived(wo.at[other_t, piece(g, k)], r_wx + 4 + k, off)
        arrived(wo.at[other_t, piece(1 - g, k)], r_wx + 6 + k, off)

    def add_head(k, h, start):
        lhs = jnp.concatenate(
            [at[k, h, 0:rows], unpack(at[k, h, rows:rows + packed].astype(f32)).astype(bf16)], axis=1)
        odd = lax.rem(h, 2)
        base = h * HV
        main = pl.ds(pl.multiple_of(base + odd * 64, 64), 128)
        side = pl.ds(pl.multiple_of(base + (1 - odd) * 128, 64), 64)
        rhs = jnp.concatenate([wo[k, main, :], wo[k, side, :], wo[k, side, :]], axis=0)
        value = jnp.dot(lhs, rhs, preferred_element_type=f32)
        if start:
            tot[...] = value
        else:
            tot[...] += value

    add_head(t, s, True)
    for h in inward:
        add_head(t, h, False)
    for h in (s,) + inward:
        arrived(at.at[other_t, h], r_a2 + h)
        add_head(other_t, h, False)
    trunk_ref[...] = (hid[...].astype(f32) + tot[...]).astype(bf16)

    for i in range(2):
        arrived(rowb.at[i], r_r + i, off | (t != i))
    for i in range(2):
        for k in range(4):
            arrived(colb.at[i, k], r_e + i * 4 + k, (t != i) | (slot != k) | (p != side))
    row_embed = (rowb[0] + rowb[1]).astype(bf16).astype(f32)
    col_embed = (colb[0] + colb[1]).reshape(4 * groups, pair).astype(bf16).astype(f32)
    summed = pin[...].astype(f32) + row_embed[:, None, :] + col_embed[None, :, :]
    flat = summed.reshape(-1, pair)
    inv = lax.rsqrt(jnp.mean(flat * flat, axis=1, keepdims=True) + EPSILON)
    normal = (flat * inv * pg[...]).astype(bf16)
    inner = gelu_tanh(jnp.dot(normal, w1[...], preferred_element_type=f32)).astype(bf16)
    update = jnp.dot(inner, w2[...], preferred_element_type=f32)
    pout_ref[...] = (flat + update).astype(bf16).reshape(pout_ref.shape)

    for copy, cond in pending:
        when(cond, lambda copy=copy: copy.wait_send())


def fused(dna_feats, conv_w, conv_gain, attn_gain, wq, wk, wv, wo, pair_w, pair_in, pair_gain, pair_w1, pair_w2):
    rows, cin = dna_feats.shape
    taps, _, half = conv_w.shape
    heads = lax.axis_size("seq")
    bf16, f32 = jnp.bfloat16, jnp.float32
    hbm = pl.BlockSpec(memory_space=pltpu.HBM)
    flat_conv = conv_w.reshape(taps * cin, half)
    pair = pair_in.shape[2]
    groups = rows // POOL
    packed = rows * HV // 128
    v = pltpu.VMEM
    scratch = [
        v(flat_conv.shape, bf16), v((half,), f32), v((half,), f32), v((2 * half,), f32),
        v((2,) + wq.shape, bf16), v((2,) + wk.shape, bf16), v((2,) + wv.shape, bf16), v((2,) + wo.shape, bf16),
        v(wo.shape, bf16), v((2,) + pair_w.shape, bf16), v(pair_in.shape, bf16), v((1, pair), f32), v(pair_w1.shape, bf16), v(pair_w2.shape, bf16),
        v((2 * rows + 2 * HALO, cin), bf16), v((2 * rows + 2 * HALO, cin), f32), v((2, rows, taps * cin), bf16),
        v((2, rows, half), f32), v((rows, half), f32), v((rows, half), bf16), v((rows, half), bf16),
        v((rows, half), bf16), v((rows, half), bf16), v((2, rows, half), bf16),
        v((heads, rows * 5 // 2, 128), bf16), v((heads, rows, QK), bf16),
        v((heads, 2, rows * 5 // 2, 128), bf16), v((heads, rows, QK), bf16),
        v((2 * heads * rows, QK), bf16), v((2 * heads * rows, 256), bf16), v((heads, packed, 128), bf16), v((2, heads, packed, 128), bf16),
        v((rows, half), f32), v(pair_w.shape, f32), v(pair_w.shape, f32), v((2, heads * 256, 2 * pair), bf16),
        v((2, groups, pair), f32), v((2, groups, pair), f32), v((2, 4, groups, pair), f32),
        pltpu.SemaphoreType.DMA((16,)), pltpu.SemaphoreType.DMA((SENDS,)), pltpu.SemaphoreType.DMA((RECVS,)),
        pltpu.SemaphoreType.REGULAR((4,)),
    ]
    return pl.pallas_call(
        fused_kernel,
        out_shape=(v((rows, half), bf16), v(pair_in.shape, bf16)),
        in_specs=[hbm] * 13,
        out_specs=(pl.BlockSpec(memory_space=v),) * 2,
        scratch_shapes=scratch,
        compiler_params=pltpu.CompilerParams(
            collective_id=0, has_side_effects=True, vmem_limit_bytes=60 * 1024 * 1024),
    )(dna_feats, flat_conv, conv_gain, attn_gain, wq, wk, wv, wo, pair_w,
      pair_in, pair_gain.reshape(1, pair), pair_w1, pair_w2)


def block(*arrays):
    dna_feats, conv_w, wq = arrays[0], arrays[1], arrays[4]
    n_seq, n_tp, n_pr = (lax.axis_size(a) for a in ("seq", "tp", "pr"))
    fits = (
        n_tp == 2 and n_pr == 2 and n_seq == 4 and lax.axis_size("grp") == 2 and wq.shape[1] == n_seq * QK
        and dna_feats.shape[0] == 128 and conv_w.shape[1] == dna_feats.shape[1]
        and arrays[3].shape[0] == 2 * conv_w.shape[2] and conv_w.shape[2] % 256 == 0
        and arrays[9].shape[0] * POOL == dna_feats.shape[0]
    )
    return fused(*arrays) if fits else local(*arrays)


def solution(mesh):
    in_specs = (
        P(("grp", "seq", "pr"), "tp"),
        P(None, "pr", "tp"),
        P("tp"),
        P(),
        P("pr", "tp"),
        P("pr", "tp"),
        P("pr", "tp"),
        P("tp", "pr"),
        P("tp", None),
        P(("grp", "seq", "tp"), "pr", None),
        P(),
        P(),
        P(),
    )
    out_specs = (P(("grp", "seq", "pr"), "tp"), P(("grp", "seq", "tp"), "pr", None))
    return jax.shard_map(block, mesh=mesh, in_specs=in_specs, out_specs=out_specs, check_vma=False)
```

```python
import math

import jax
import jax.numpy as jnp
from jax import lax
from jax.experimental import pallas as pl
from jax.experimental.pallas import tpu as pltpu
from jax.sharding import PartitionSpec as P

QK = 128
HV = 192
POOL = 16


EPSILON = 1e-06


def extended(value, sides, width):
    for axis, dim in sides:
        devices, length = (lax.axis_size(axis), value.shape[dim])
        up = [(i, (i + 1) % devices) for i in range(devices - 1)]
        down = [(j, i) for i, j in up]
        last = lax.slice_in_dim(value, length - width, length, axis=dim)
        first = lax.slice_in_dim(value, 0, width, axis=dim)
        before = lax.ppermute(last, axis, up)
        after = lax.ppermute(first, axis, down)
        value = jnp.concatenate([before, value, after], axis=dim)
    return value


def rms_scale(values):
    return lax.rsqrt(jnp.mean(values * values, axis=-1, keepdims=True) + EPSILON)


def attention_start(query_block):
    head_count = query_block.shape[1]
    row_count = query_block.shape[0]
    highest = jnp.full((head_count, row_count), -1e30, jnp.float32)
    totals = jnp.zeros((head_count, row_count), jnp.float32)
    mixed = jnp.zeros((row_count, head_count, HV), jnp.float32)
    return (highest, totals, mixed)


def attention_step(query_block, carry, pieces):
    factor = 1.0 / math.sqrt(QK)
    highest, totals, mixed = carry
    key_piece, value_piece = pieces
    scores = (
        jnp.einsum("qhd,khd->hqk", query_block, key_piece, preferred_element_type=jnp.float32)
        * factor
    )
    new_high = jnp.maximum(highest, jnp.max(scores, axis=-1))
    weights = jnp.exp(scores - new_high[:, :, None])
    totals = jnp.sum(weights, axis=-1)
    added = jnp.einsum(
        "hqk,khd->qhd",
        weights.astype(jnp.bfloat16),
        value_piece,
        preferred_element_type=jnp.float32,
    )
    mixed = added
    return (new_high, totals, mixed)


def attention_finish(carry):
    highest, totals, mixed = carry
    return (mixed / jnp.transpose(totals)[:, :, None]).astype(jnp.bfloat16)


def local(
    dna_feats,
    conv_w,
    conv_gain,
    attn_gain,
    wq,
    wk,
    wv,
    wo,
    pair_w,
    pair_in,
    pair_gain,
    pair_w1,
    pair_w2,
):
    row_count = dna_feats.shape[0]
    reach = conv_w.shape[0] // 2
    rimmed = extended(dna_feats, ((("seq", "pr"), 0),), reach)
    channels = lax.all_gather(rimmed, "tp", axis=1, tiled=True)
    conv_empty = jnp.zeros((row_count, conv_w.shape[2]), jnp.float32)
    total = conv_empty
    piece = lax.all_gather(conv_w, "pr", axis=1, tiled=True)
    sliced = channels
    for offset in range(piece.shape[0]):
        total = total + jnp.dot(
            sliced[offset : offset + row_count], piece[offset], preferred_element_type=jnp.float32
        )
    squares = lax.psum(jnp.sum(total * total, axis=1, keepdims=True), "tp")
    model_width = total.shape[1] * lax.axis_size("tp")
    hidden_conv = jax.nn.gelu(
        total * lax.rsqrt(squares / model_width + EPSILON) * conv_gain
    ).astype(jnp.bfloat16)
    trunk_full = lax.all_gather(hidden_conv, "tp", axis=1, tiled=True)
    trunk_wide = trunk_full.astype(jnp.float32)
    normed = (trunk_wide * rms_scale(trunk_wide) * attn_gain).astype(jnp.bfloat16)
    query_width = wq.shape[1]
    pieces = (
        lax.all_gather(wq, "pr", axis=0, tiled=True),
        lax.all_gather(wk, "pr", axis=0, tiled=True),
        lax.all_gather(wv, "pr", axis=0, tiled=True),
    )
    sliced = normed
    query_sum, key_sum, value_sum = tuple(
        (jnp.dot(sliced, piece, preferred_element_type=jnp.float32) for piece in pieces)
    )
    head_count = query_width // QK
    queries = query_sum.astype(jnp.bfloat16).reshape(row_count, head_count, QK)
    keys_local = key_sum.astype(jnp.bfloat16).reshape(row_count, head_count, QK)
    values_local = value_sum.astype(jnp.bfloat16).reshape(row_count, head_count, HV)
    moved_query, moved_keys, moved_values = (
        lax.all_to_all(queries, "pr", split_axis=1, concat_axis=0, tiled=True),
        lax.all_to_all(keys_local, "pr", split_axis=1, concat_axis=0, tiled=True),
        lax.all_to_all(values_local, "pr", split_axis=1, concat_axis=0, tiled=True),
    )
    carried = attention_step(
        moved_query,
        attention_start(moved_query),
        (
            lax.all_gather(moved_keys, "seq", axis=0, tiled=True),
            lax.all_gather(moved_values, "seq", axis=0, tiled=True),
        ),
    )
    attended = lax.all_to_all(
        attention_finish(carried), "pr", split_axis=0, concat_axis=1, tiled=True
    )
    attended_flat = attended.reshape(row_count, head_count * HV)
    head_terms = jnp.dot(
        attended_flat,
        lax.all_gather(wo, "pr", axis=1, tiled=True),
        preferred_element_type=jnp.float32,
    )
    own_share = lax.psum_scatter(
        head_terms.astype(jnp.bfloat16), "tp", scatter_dimension=1, tiled=True
    ).astype(jnp.float32)
    trunk = (hidden_conv.astype(jnp.float32) + own_share).astype(jnp.bfloat16)
    pooled = trunk.astype(jnp.float32).reshape(row_count // POOL, POOL, -1).mean(axis=1)
    partial_embed = jnp.dot(pooled, pair_w.astype(jnp.float32), precision=lax.Precision.HIGHEST)
    embedded = lax.psum(partial_embed, "tp").astype(jnp.bfloat16)
    every_embed = lax.all_gather(embedded, ("seq", "pr"), axis=0, tiled=True)
    pair_rows = pair_in.shape[0]
    pair_cols = pair_in.shape[1]
    pair_width = pair_in.shape[2]
    row_first = lax.axis_index(("seq", "tp")) * pair_rows
    col_first = lax.axis_index("pr") * pair_cols
    row_embed = lax.dynamic_slice_in_dim(every_embed, row_first, pair_rows, 0)[
        :, :pair_width
    ].astype(jnp.float32)
    col_embed = lax.dynamic_slice_in_dim(every_embed, col_first, pair_cols, 0)[
        :, pair_width:
    ].astype(jnp.float32)
    summed = pair_in.astype(jnp.float32) + row_embed[:, None, :] + col_embed[None, :, :]
    pair_normed = (summed * rms_scale(summed) * pair_gain).astype(jnp.bfloat16)
    inner = jax.nn.gelu(
        jnp.dot(pair_normed.reshape(-1, pair_width), pair_w1, preferred_element_type=jnp.float32)
    ).astype(jnp.bfloat16)
    update = jnp.dot(inner, pair_w2, preferred_element_type=jnp.float32).reshape(summed.shape)
    pair_out = (summed + update).astype(jnp.bfloat16)
    return (trunk, pair_out)


def gelu_tanh(x):
    return 0.5 * x * (1.0 + jnp.tanh(math.sqrt(2.0 / math.pi) * (x + 0.044715 * (x * x * x))))


class Sems:
    def __init__(self, ref, limit):
        self.ref, self.limit, self.used = ref, limit, 0

    def take(self, count=1):
        first = self.used
        self.used += count
        assert self.used <= self.limit
        return first


SENDS = 25
RECVS = 50
HALO = 16
SIZES = (64, 64)
CHUNKS = len(SIZES)
STARTS = tuple(sum(SIZES[:i]) for i in range(CHUNKS))


def fused_kernel(
    x_hbm, cw_hbm, cg_hbm, ag_hbm, wq_hbm, wk_hbm, wv_hbm, wo_hbm, pw_hbm, pin_hbm, pg_hbm, w1_hbm, w2_hbm,
    trunk_ref, pout_ref,
    cw, cg, cgo, ag, wq, wk, wv, wo, wl, pw, pin, pg, w1, w2,
    xin, xf, im, acc, accr, cvt, cvr, hid, hoth, nrm,
    kvo, qo, kvb, qb, kf, vf, ao, at, tot, mp, mr, mb, eb, rowb, colb,
    lsem, ssem, rsem, rel,
):
    s, t, p = lax.axis_index("seq"), lax.axis_index("tp"), lax.axis_index("pr")
    g = lax.axis_index("grp")
    n_seq = 4
    rows, cin = x_hbm.shape
    half = hid.shape[1]
    width = 2 * half
    sends, recvs, locals_ = Sems(ssem, SENDS), Sems(rsem, RECVS), Sems(lsem, 14)
    pending = []
    f32, bf16 = jnp.float32, jnp.bfloat16
    other_t, other_p = 1 - t, 1 - p
    diag, off = p == t, p != t
    partner, across, beside = {"pr": other_p}, {"tp": other_t}, {"grp": 1 - g}

    def when(cond, run):
        if cond is None:
            run()
        else:
            pl.when(cond)(run)

    teams = {}

    def remote(src, dst, recv, dev, cond=None, team=None):
        number = sends.take() if team not in teams else teams[team]
        copy = pltpu.make_async_remote_copy(
            src_ref=src, dst_ref=dst, send_sem=ssem.at[number], recv_sem=rsem.at[recv],
            device_id=dev, device_id_type=pl.DeviceIdType.MESH,
        )
        when(cond, lambda: copy.start())
        if team is None:
            pending.append((copy, cond))
        else:
            teams[team] = number

    def settle(team, whole, cond=None):
        copy = pltpu.make_async_remote_copy(
            src_ref=whole, dst_ref=whole, send_sem=ssem.at[teams[team]], recv_sem=rsem.at[0],
            device_id=partner, device_id_type=pl.DeviceIdType.MESH,
        )
        when(cond, lambda: copy.wait_send())

    def arrived(dst, recv, cond=None):
        copy = pltpu.make_async_remote_copy(
            src_ref=dst, dst_ref=dst, send_sem=ssem.at[0], recv_sem=rsem.at[recv],
            device_id=partner, device_id_type=pl.DeviceIdType.MESH,
        )
        when(cond, lambda: copy.wait_recv())

    def signal(sem, dev, cond=None):
        when(cond, lambda: pl.semaphore_signal(sem, inc=1, device_id=dev, device_id_type=pl.DeviceIdType.MESH))

    def load(src, dst, cond=None):
        copy = pltpu.make_async_copy(src, dst, lsem.at[locals_.take()])
        when(cond, lambda: copy.start())
        return lambda: when(cond, lambda: copy.wait())

    barrier = pltpu.get_barrier_semaphore()
    has_up, has_down = s < n_seq - 1, s > 0
    up, down = lax.rem(s + 1, n_seq), lax.rem(s + n_seq - 1, n_seq)
    signal(barrier, across)
    signal(barrier, {"tp": other_t, "pr": other_p})
    signal(barrier, beside)
    signal(barrier, {"seq": up}, has_up)
    signal(barrier, {"seq": down}, has_down)
    signal(barrier, {"seq": up, "tp": p, "pr": 0}, has_up)
    signal(barrier, {"seq": down, "tp": p, "pr": 1}, has_down)
    signal(barrier, partner)

    mine = pl.ds(pl.multiple_of(HALO + p * rows, HALO), rows)
    got_x = load(x_hbm, xin.at[mine], diag)
    got_cw = load(cw_hbm, cw)
    got_gain = [load(cg_hbm, cg), load(ag_hbm, ag)]
    got_w = [load(wk_hbm, wk.at[p]), load(wv_hbm, wv.at[p]), load(wq_hbm, wq.at[p])]
    got_wo = load(wo_hbm, wo.at[t], diag)
    got_local = [load(wo_hbm, wl), load(pw_hbm, pw.at[t])]
    got_late = [ load(pin_hbm, pin), load(pg_hbm, pg), load(w1_hbm, w1), load(w2_hbm, w2)]

    ups, downs = has_up.astype(jnp.int32), has_down.astype(jnp.int32)
    pl.semaphore_wait(barrier, 4 + ups + downs + 2 * p * ups + 2 * (1 - p) * downs)

    first_rows = SIZES[0] + HALO
    portions = [(0, first_rows), (rows - HALO, HALO), (first_rows, rows - HALO - first_rows)]
    if first_rows > rows - HALO - HALO:
        portions = [(0, rows)]
    early = max(1, len(portions) - 1)
    r_x = recvs.take(2 * len(portions) + 2)
    r_halo = r_x + 2 * len(portions)

    def portion(q, first, count):
        return xin.at[pl.ds(pl.multiple_of(HALO + q * rows + first, HALO), count)]

    def send_x(index):
        first, count = portions[index]
        for td in (other_t, t):
            remote(x_hbm.at[pl.ds(first, count)], portion(p, first, count), r_x + p * len(portions) + index,
                   {"tp": td, "pr": t}, None if td is other_t else off,
                   "input across" if td is other_t else "input")

    for index in range(early):
        send_x(index)
    for td in (other_t, t):
        low, high = xin.at[pl.ds(0, HALO)], xin.at[pl.ds(HALO + 2 * rows, HALO)]
        remote(x_hbm.at[pl.ds(rows - HALO, HALO)], low, r_halo, {"seq": up, "tp": td, "pr": t}, (p == 1) & has_up, "rim up")
        remote(x_hbm.at[pl.ds(0, HALO)], high, r_halo + 1, {"seq": down, "tp": td, "pr": t}, (p == 0) & has_down, "rim down")
    for index in range(early, len(portions)):
        send_x(index)
    r_g, r_w, r_wo, r_wx, r_pw, r_m = recvs.take(), recvs.take(3), recvs.take(), recvs.take(5), recvs.take(2), recvs.take()
    remote(cg_hbm, cgo, r_g, across)
    def piece(group, k):
        return pl.ds(pl.multiple_of(group * (half // 2) + k * (half // 4), half // 4), half // 4)

    def relay(k):
        block = wo.at[other_t, piece(g, k)]
        arrived(block, r_wx + k, diag)
        remote(block, block, r_wx + 2 + k, beside, diag, "wo beside")
        remote(block, block, r_wx + 4, partner, diag, "wo on")

    def hand_over(k):
        block = wo.at[other_t, piece(1 - g, k)]
        arrived(block, r_wx + 2 + k, diag)
        remote(block, block, r_wx + 4, partner, diag, "wo on")

    part = pl.ds(pl.multiple_of(g * (half // 2), half // 2), half // 2)
    rest = pl.ds(pl.multiple_of((1 - g) * (half // 2), half // 2), half // 2)
    remote(wk_hbm, wk.at[p], r_w, partner, None, "qk")
    remote(wv_hbm, wv.at[p], r_w + 1, partner)
    both = has_up & has_down
    signal(rel.at[0], {"seq": up}, both)
    signal(rel.at[1], {"seq": down}, both)

    @pl.when(s == 0)
    def _():
        xin[pl.ds(0, HALO), :] = jnp.zeros((HALO, cin), bf16)

    @pl.when(s == n_seq - 1)
    def _():
        xin[pl.ds(HALO + 2 * rows, HALO), :] = jnp.zeros((HALO, cin), bf16)

    got_x()
    taps = im.shape[2] // cin
    spans = [pl.ds(first, count) for first, count in zip(STARTS, SIZES)]
    step = 256
    r_c, r_v = recvs.take(CHUNKS), recvs.take(CHUNKS)

    def take_x(indices):
        for q in range(2):
            for index in indices:
                first, count = portions[index]
                arrived(portion(q, first, count), r_x + q * len(portions) + index, off | (p != q))

    def convolve(c):
        start, size = STARTS[c], SIZES[c]
        for q in range(2):
            base = HALO + q * rows + start
            window = pl.ds(base - HALO, size + 2 * HALO)
            xf[window, :] = xin[window, :].astype(f32)
            for o in range(taps):
                im[q, spans[c], o * cin:(o + 1) * cin] = xf[pl.ds(base - taps // 2 + o, size), :].astype(bf16)
        for first in range(0, half, 384):
            cols = pl.ds(first, 384)
            value = jnp.dot(im[:, spans[c], :].reshape(2 * size, taps * cin), cw[:, cols], preferred_element_type=f32)
            acc[:, spans[c], cols] = value.reshape(2, size, 384)
        remote(acc.at[other_p, spans[c]], accr.at[spans[c]], r_c + c, partner, None, "sums")

    def exchange(c):
        arrived(accr.at[spans[c]], r_c + c)
        value = acc[p, spans[c]] + accr[spans[c]]
        accr[spans[c]] = value
        cvt[spans[c]] = value.astype(bf16)
        remote(cvt.at[spans[c]], cvr.at[spans[c]], r_v + c, across, None, "conv")

    take_x(range(early))
    arrived(xin.at[pl.ds(0, HALO)], r_halo, has_down)
    if CHUNKS == 1 or early == len(portions):
        arrived(xin.at[pl.ds(HALO + 2 * rows, HALO)], r_halo + 1, has_up)
    got_cw()
    convolve(0)
    if CHUNKS > 1 and early < len(portions):
        arrived(xin.at[pl.ds(HALO + 2 * rows, HALO)], r_halo + 1, has_up)
    take_x(range(early, len(portions)))
    remote(pw_hbm.at[part], pw.at[t, part], r_pw, across, diag)
    for c in range(1, CHUNKS):
        convolve(c)
        exchange(c - 1)
    exchange(CHUNKS - 1)
    arrived(pw.at[other_t, part], r_pw, off)
    remote(pw.at[other_t, part], pw.at[other_t, part], r_pw + 1, beside, off)
    remote(wq_hbm, wq.at[p], r_w + 2, partner, None, "qk")
    remote(wo_hbm, wo.at[t], r_wo, partner, diag)

    when(s >= 2, lambda: pl.semaphore_wait(rel.at[0], 1))
    when(s <= 1, lambda: pl.semaphore_wait(rel.at[1], 1))
    signal(rel.at[2], {"seq": 3}, s == 2)
    signal(rel.at[3], {"seq": 0}, s == 1)
    when(s == 3, lambda: pl.semaphore_wait(rel.at[2], 1))
    when(s == 0, lambda: pl.semaphore_wait(rel.at[3], 1))

    for wait in got_gain + got_w:
        wait()
    arrived(cgo, r_g)
    low_gain, high_gain = ag[pl.ds(0, half)][None, :], ag[pl.ds(half, half)][None, :]
    gains = [jnp.where(t == 0, low_gain, high_gain), jnp.where(t == 0, high_gain, low_gain)]
    conv_gains = [cg[...][None, :], cgo[...][None, :]]

    def normalize(c):
        span = spans[c]
        size = SIZES[c]
        arrived(cvr.at[span], r_v + c)
        square = jnp.zeros((size, 1), f32)
        for first in range(0, half, step):
            cols = pl.ds(first, step)
            own, other = accr[span, cols], cvr[span, cols].astype(f32)
            square = square + jnp.sum(own * own + other * other, axis=1, keepdims=True)
        scale = lax.rsqrt(square / width + EPSILON)
        square = jnp.zeros((size, 1), f32)
        for first in range(0, half, step):
            cols = pl.ds(first, step)
            for source, target, gain in ((accr, hid, conv_gains[0]), (cvr, hoth, conv_gains[1])):
                rounded = gelu_tanh(source[span, cols].astype(f32) * scale * gain[:, first:first + step]).astype(bf16)
                target[span, cols] = rounded
                back = rounded.astype(f32)
                square = square + jnp.sum(back * back, axis=1, keepdims=True)
        scale = lax.rsqrt(square / width + EPSILON)
        for first in range(0, half, step):
            cols = pl.ds(first, step)
            for source, place, gain in ((hid, t, gains[0]), (hoth, other_t, gains[1])):
                nrm[place, span, cols] = (
                    source[span, cols].astype(f32) * scale * gain[:, first:first + step]).astype(bf16)

    near1 = s + 1 - 2 * lax.rem(s, 2)
    near2 = jnp.where(s < 2, 2, 1)
    near3 = jnp.where(s < 2, 3, 0)
    outward = (near2, near3, near1)
    inward = (near1, near2, near3)
    r_kv, r_kv2, r_q = recvs.take(n_seq * CHUNKS), recvs.take(CHUNKS), recvs.take(n_seq)
    low_lanes = lax.broadcasted_iota(jnp.int32, (1, 128), 1) < 64

    def rows_of(c):
        start, size = STARTS[c], SIZES[c]
        return start * 5 // 2, size, size // 2, pl.ds(start * 5 // 2, size * 5 // 2)

    def project(c, weights, first, count):
        value = jnp.dot(nrm[0, spans[c]], weights[0, :, first:first + count], preferred_element_type=f32)
        return value + jnp.dot(nrm[1, spans[c]], weights[1, :, first:first + count], preferred_element_type=f32)

    def keys_values(c):
        base, size, tall, whole = rows_of(c)
        main_rows, side_rows = pl.ds(base + size, size), pl.ds(base + 2 * size, tall)
        for first in range(0, n_seq * QK, step):
            value = project(c, wk, first, step)
            for k in range(step // QK):
                kvo[first // QK + k, base:base + size] = value[:, k * QK:(k + 1) * QK].astype(bf16)
        for m in range(n_seq // 2):
            value = project(c, wv, m * 384, 384)
            main0, shared, main1 = value[:, :128], value[:, 128:256], value[:, 256:]
            turned = pltpu.roll(shared, 64, 1)
            kvo[2 * m, main_rows] = main0.astype(bf16)
            kvo[2 * m + 1, main_rows] = main1.astype(bf16)
            kvo[2 * m, side_rows] = jnp.where(low_lanes, shared[:tall], turned[tall:]).astype(bf16)
            kvo[2 * m + 1, side_rows] = jnp.where(low_lanes, turned[:tall], shared[tall:]).astype(bf16)
        for h in outward:
            remote(kvo.at[h, whole], kvb.at[s, p, whole], r_kv + s * CHUNKS + c, {"seq": h}, None, "kv")
        remote(kvo.at[s, whole], kvb.at[s, p, whole], r_kv2 + c, partner, None, "kv")
        kvb[s, p, whole] = kvo[s, whole]

    def queries():
        for first in range(0, n_seq * QK, step):
            value = sum(jnp.dot(nrm[k], wq[k, :, first:first + step], preferred_element_type=f32) for k in range(2))
            for k in range(step // QK):
                qo[first // QK + k] = value[:, k * QK:(k + 1) * QK].astype(bf16)
        for h in outward:
            remote(qo.at[h], qb.at[s], r_q + s, {"seq": h}, None, "q")
        qb[s] = qo[s]

    for c in range(CHUNKS):
        normalize(c)
        if c == 0:
            arrived(wk.at[other_p], r_w)
            arrived(wv.at[other_p], r_w + 1)
        keys_values(c)
        if c == 0:
            for k in range(2):
                remote(wo_hbm.at[piece(g, k)], wo.at[t, piece(g, k)], r_wx + k, across, off, "wo across")
    arrived(wq.at[other_p], r_w + 2)
    queries()

    groups = rows // POOL
    pair = pin.shape[2]

    def split(value):
        high = value.astype(bf16)
        left = value - high.astype(f32)
        second = left.astype(bf16)
        return high, second, (left - second.astype(f32)).astype(bf16)

    def pool(value):
        return jnp.sum(value.reshape(value.shape[0] // POOL, POOL, value.shape[1]), axis=1) * (1.0 / POOL)

    def spread(j, q, c):
        base, size, tall, _ = rows_of(c)
        place = 2 * n_seq * STARTS[c] + (j * 2 + q) * size
        kf[pl.ds(pl.multiple_of(place, 32), size), :] = kvb[j, q, base:base + size]
        vf[pl.ds(pl.multiple_of(place, 32), size), 0:128] = kvb[j, q, base + size:base + 2 * size]
        extra = kvb[j, q, base + 2 * size:base + 2 * size + tall].astype(f32)
        vf[pl.ds(pl.multiple_of(place, 16), tall), 128:256] = jnp.where(low_lanes, extra, 0.0).astype(bf16)
        vf[pl.ds(pl.multiple_of(place + tall, 16), tall), 128:256] = jnp.where(low_lanes, 0.0, extra).astype(bf16)

    relay(0)
    for c in range(CHUNKS):
        spread(s, p, c)
        for j in inward:
            arrived(kvb.at[j, p, rows_of(c)[3]], r_kv + j * CHUNKS + c)
            remote(kvb.at[j, p, rows_of(c)[3]], kvb.at[j, p, rows_of(c)[3]], r_kv2 + c, partner, None, "kv on")
            spread(j, p, c)
        if c == 0:
            for wait in got_local:
                wait()
            arrived(pw.at[other_t, rest], r_pw + 1, off)
            mp[...] = jnp.dot(wl[...], pw[p], preferred_element_type=f32)
            remote(mp, mr, r_m, partner)
            own_embed = jnp.zeros((groups, 2 * pair), f32)
            for part3 in split(pool(hid[...].astype(f32)))[::-1]:
                own_embed = own_embed + jnp.dot(part3, pw[t], preferred_element_type=f32)
            relay(1)
    for c in range(CHUNKS):
        arrived(kvb.at[:, other_p, rows_of(c)[3]], r_kv2 + c)
        for j in range(n_seq):
            spread(j, other_p, c)

    factor = 1.0 / math.sqrt(QK)
    r_a, r_a2 = recvs.take(n_seq), recvs.take(n_seq)
    packed = rows // 2

    def attend(j):
        if j is not s:
            arrived(qb.at[j], r_q + j)
        scores = lax.dot_general(
            qb[j], kf[...],
            (((1,), (1,)), ((), ())), preferred_element_type=f32) * factor
        weights = jnp.exp(scores - jnp.max(scores, axis=1, keepdims=True))
        sums = jnp.sum(weights, axis=1, keepdims=True)
        mixed = jnp.dot(weights.astype(bf16), vf[...], preferred_element_type=f32) / sums
        extra = mixed[:, 128:]
        extra = extra + pltpu.roll(extra, 64, 1)
        out = at.at[t, s] if j is s else ao.at[j]
        out[0:rows, :] = mixed[:, :128].astype(bf16)
        out[rows:rows + packed, :] = jnp.where(low_lanes, extra[:packed], extra[packed:]).astype(bf16)
        if j is s:
            remote(at.at[t, s], at.at[t, s], r_a2 + s, across, None, "result on")
        else:
            remote(ao.at[j], at.at[t, s], r_a + s, {"seq": j}, None, "result")

    for j in (near2, near3, near1):
        attend(j)
    attend(s)

    arrived(mr, r_m)
    for h in range(n_seq):
        odd = h % 2
        main, side = h * HV + odd * 64, h * HV + (1 - odd) * 128
        for first, count, source in ((0, 128, main), (128, 64, side), (192, 64, side)):
            value = mp[pl.ds(source, count), :] + mr[pl.ds(source, count), :]
            high = value.astype(bf16)
            place = pl.ds(h * 256 + first, count)
            mb[0, place, :] = high
            mb[1, place, :] = (value - high.astype(f32)).astype(bf16)

    def unpack(extra):
        return jnp.concatenate([jnp.where(low_lanes, extra, 0.0), jnp.where(low_lanes, 0.0, extra)], axis=0)

    def contribution(h):
        place = pl.ds(pl.multiple_of(h * 256, 256), 256)
        pooled = jnp.concatenate([
            pool(at[t, h, 0:rows].astype(f32)), unpack(pool(at[t, h, rows:rows + packed].astype(f32)))], axis=1)
        high, second, third = split(pooled)
        fine = jnp.dot(jnp.concatenate([second, high], axis=0), mb[1, place, :], preferred_element_type=f32)
        coarse = jnp.dot(jnp.concatenate([third, second, high], axis=0), mb[0, place, :], preferred_element_type=f32)
        fine = fine[:groups] + fine[groups:]
        return (fine + coarse[:groups]) + (coarse[groups:2 * groups] + coarse[2 * groups:])

    embed = own_embed + contribution(s)
    for h in inward:
        arrived(at.at[t, h], r_a + h)
        remote(at.at[t, h], at.at[t, h], r_a2 + h, across, None, "result on")
        embed = embed + contribution(h)
    eb[0] = embed[:, :pair]
    eb[1] = embed[:, pair:]
    r_r, r_e = recvs.take(2), recvs.take()
    side = s // 2
    slot = lax.rem(s, 2) * 2 + p
    for h in outward + (s,):
        for dt in range(2):
            here = h is s and dt == 0
            remote(eb.at[1], colb.at[t * 4 + slot], r_e, {"seq": h, "tp": lax.rem(t + dt, 2), "pr": side},
                   (p != side) if here else None, None if here else "column")
    remote(eb.at[0], rowb.at[t], r_r + t, {"tp": p, "pr": other_p})
    remote(eb.at[0], rowb.at[t], r_r + t, {"tp": p}, off)

    @pl.when(diag)
    def _():
        rowb[t] = eb[0]

    @pl.when(p == side)
    def _():
        colb[t * 4 + slot] = eb[1]

    hand_over(0)
    hand_over(1)
    arrived(wo.at[t], r_wo, off)
    got_wo()
    for wait in got_late:
        wait()
    arrived(wo.at[other_t], r_wx + 4, off)

    def add_head(k, h, start):
        lhs = jnp.concatenate(
            [at[k, h, 0:rows], unpack(at[k, h, rows:rows + packed].astype(f32)).astype(bf16)], axis=1)
        odd = lax.rem(h, 2)
        base = h * HV
        main = pl.ds(pl.multiple_of(base + odd * 64, 64), 128)
        side = pl.ds(pl.multiple_of(base + (1 - odd) * 128, 64), 64)
        rhs = jnp.concatenate([wo[k, main, :], wo[k, side, :], wo[k, side, :]], axis=0)
        value = jnp.dot(lhs, rhs, preferred_element_type=f32)
        if start:
            tot[...] = value
        else:
            tot[...] += value

    add_head(t, s, True)
    for h in inward:
        add_head(t, h, False)
    for h in (s,) + inward:
        arrived(at.at[other_t, h], r_a2 + h)
        add_head(other_t, h, False)
    trunk_ref[...] = (hid[...].astype(f32) + tot[...]).astype(bf16)

    for i in range(2):
        arrived(rowb.at[i], r_r + i, off | (t != i))
    arrived(colb.at[pl.ds(0, 7)], r_e, p == side)
    arrived(colb, r_e, p != side)
    row_embed = (rowb[0] + rowb[1]).astype(bf16).astype(f32)
    col_embed = (colb[0:4] + colb[4:8]).reshape(4 * groups, pair).astype(bf16).astype(f32)
    summed = pin[...].astype(f32) + row_embed[:, None, :] + col_embed[None, :, :]
    flat = summed.reshape(-1, pair)
    inv = lax.rsqrt(jnp.mean(flat * flat, axis=1, keepdims=True) + EPSILON)
    normal = (flat * inv * pg[...]).astype(bf16)
    inner = gelu_tanh(jnp.dot(normal, w1[...], preferred_element_type=f32)).astype(bf16)
    update = jnp.dot(inner, w2[...], preferred_element_type=f32)
    pout_ref[...] = (flat + update).astype(bf16).reshape(pout_ref.shape)

    for team, whole, cond in (
            ("input across", xin.at[mine], None), ("input", xin.at[mine], off),
            ("rim up", xin.at[pl.ds(0, 2 * HALO)], (p == 1) & has_up),
            ("rim down", xin.at[pl.ds(0, 2 * HALO)], (p == 0) & has_down),
            ("sums", accr, None), ("conv", cvt, None), ("qk", wk, None), ("kv", kvo, None), ("q", qo.at[pl.ds(0, 3)], None),
            ("kv on", kvo.at[pl.ds(0, 3)], None), ("wo across", wo.at[t, part], off), ("wo beside", wo.at[t, part], diag),
            ("wo on", wo.at[t], diag), ("result", ao.at[pl.ds(0, 3)], None), ("result on", at.at[t], None),
            ("column", colb.at[pl.ds(0, 7)], None)):
        settle(team, whole, cond)
    for copy, cond in pending:
        when(cond, lambda copy=copy: copy.wait_send())


def fused(dna_feats, conv_w, conv_gain, attn_gain, wq, wk, wv, wo, pair_w, pair_in, pair_gain, pair_w1, pair_w2):
    rows, cin = dna_feats.shape
    taps, _, half = conv_w.shape
    heads = lax.axis_size("seq")
    bf16, f32 = jnp.bfloat16, jnp.float32
    hbm = pl.BlockSpec(memory_space=pltpu.HBM)
    flat_conv = conv_w.reshape(taps * cin, half)
    pair = pair_in.shape[2]
    groups = rows // POOL
    packed = rows * HV // 128
    v = pltpu.VMEM
    scratch = [
        v(flat_conv.shape, bf16), v((half,), f32), v((half,), f32), v((2 * half,), f32),
        v((2,) + wq.shape, bf16), v((2,) + wk.shape, bf16), v((2,) + wv.shape, bf16), v((2,) + wo.shape, bf16),
        v(wo.shape, bf16), v((2,) + pair_w.shape, bf16), v(pair_in.shape, bf16), v((1, pair), f32), v(pair_w1.shape, bf16), v(pair_w2.shape, bf16),
        v((2 * rows + 2 * HALO, cin), bf16), v((2 * rows + 2 * HALO, cin), f32), v((2, rows, taps * cin), bf16),
        v((2, rows, half), f32), v((rows, half), f32), v((rows, half), bf16), v((rows, half), bf16),
        v((rows, half), bf16), v((rows, half), bf16), v((2, rows, half), bf16),
        v((heads, rows * 5 // 2, 128), bf16), v((heads, rows, QK), bf16),
        v((heads, 2, rows * 5 // 2, 128), bf16), v((heads, rows, QK), bf16),
        v((2 * heads * rows, QK), bf16), v((2 * heads * rows, 256), bf16), v((heads, packed, 128), bf16), v((2, heads, packed, 128), bf16),
        v((rows, half), f32), v(pair_w.shape, f32), v(pair_w.shape, f32), v((2, heads * 256, 2 * pair), bf16),
        v((2, groups, pair), f32), v((2, groups, pair), f32), v((8, groups, pair), f32),
        pltpu.SemaphoreType.DMA((14,)), pltpu.SemaphoreType.DMA((SENDS,)), pltpu.SemaphoreType.DMA((RECVS,)),
        pltpu.SemaphoreType.REGULAR((4,)),
    ]
    return pl.pallas_call(
        fused_kernel,
        out_shape=(v((rows, half), bf16), v(pair_in.shape, bf16)),
        in_specs=[hbm] * 13,
        out_specs=(pl.BlockSpec(memory_space=v),) * 2,
        scratch_shapes=scratch,
        compiler_params=pltpu.CompilerParams(
            collective_id=0, has_side_effects=True, vmem_limit_bytes=60 * 1024 * 1024),
    )(dna_feats, flat_conv, conv_gain, attn_gain, wq, wk, wv, wo, pair_w,
      pair_in, pair_gain.reshape(1, pair), pair_w1, pair_w2)


def block(*arrays):
    dna_feats, conv_w, wq = arrays[0], arrays[1], arrays[4]
    n_seq, n_tp, n_pr = (lax.axis_size(a) for a in ("seq", "tp", "pr"))
    fits = (
        n_tp == 2 and n_pr == 2 and n_seq == 4 and lax.axis_size("grp") == 2 and wq.shape[1] == n_seq * QK
        and dna_feats.shape[0] == 128 and conv_w.shape[1] == dna_feats.shape[1]
        and arrays[3].shape[0] == 2 * conv_w.shape[2] and conv_w.shape[2] % 256 == 0
        and arrays[9].shape[0] * POOL == dna_feats.shape[0]
    )
    return fused(*arrays) if fits else local(*arrays)


def solution(mesh):
    in_specs = (
        P(("grp", "seq", "pr"), "tp"),
        P(None, "pr", "tp"),
        P("tp"),
        P(),
        P("pr", "tp"),
        P("pr", "tp"),
        P("pr", "tp"),
        P("tp", "pr"),
        P("tp", None),
        P(("grp", "seq", "tp"), "pr", None),
        P(),
        P(),
        P(),
    )
    out_specs = (P(("grp", "seq", "pr"), "tp"), P(("grp", "seq", "tp"), "pr", None))
    return jax.shard_map(block, mesh=mesh, in_specs=in_specs, out_specs=out_specs, check_vma=False)
```
